128 devices in a mesh: query: 4 (over z_lo, core), lib: 32 (over x, y, z_hi).
Axes of the slice: x: 4, y: 4, z: 4 (z_hi: 2, z_lo: 2; z = z_hi * 2 + z_lo), core: 2. Of those that a mesh axis runs over, the one named last changes fastest.
Arguments:
- queries: bfloat16 [4096, 2048], P(('query', 'lib')), may hold values from -64 to 64
- query_bucket: int32 [4096], P(('query', 'lib')), may hold values from 0 to 63, as said below
- library: bfloat16 [98304, 2048], P(('lib', 'query')), may hold values from -64 to 64
- library_time: bfloat16 [98304], P(('lib', 'query')), may hold values from 0 to 2
- library_bucket: int32 [98304], P(('lib', 'query')), may hold values from 0 to 63, as said below
Outputs:
- expected_spectra: bfloat16 [4096, 2048], P(('query', 'lib'))
- expected_time: float32 [4096], P(('query', 'lib'))
- log_evidence: float32 [4096], P(('query', 'lib'))
The draws below stay inside these ranges and needn't reach their ends.
Inputs may be any that keep to these rules, and one draw needn't show every extreme that they name: `query_bucket`: library entries whose bucket differs from a query's by at most one are that query's candidates; the queries held by the devices at index i of lib lie in buckets 2 i and 2 i + 1. `library_bucket`: the library entries of every device hold each of the 64 buckets exactly 3072 // 256 times.
All inputs are finite; a program needn't handle non-finite values.
Results may differ from the reference program's by a relative error of at most 0.003.
Values may be sent and summed in bfloat16 or wider, within the bound.
A program may use at most 128 MiB of HBM per device.

```python
from functools import partial
import jax
import jax.numpy as jnp
from jax import lax

BINS = 2048
QUERY_DEV = 32
ENTRY_DEV = 3072
SHARPNESS = 448
BUCKETS = 64
QUERIES = 4096
ENTRIES = 98304
BLOCK_ROWS = 1024
N_QUERY = 4
N_LIB = 32


def raw_row(base, index):
    return jnp.clip(jax.random.normal(jax.random.fold_in(base, index), (BINS,), jnp.float32), -5.0, 5.0)


def block_permutation(base, index):
    return jax.random.permutation(jax.random.fold_in(base, index), ENTRY_DEV // N_QUERY)


def entry_permutations(key):
    per_device = ENTRY_DEV // N_QUERY
    return jax.vmap(partial(block_permutation, jax.random.fold_in(key, 12)))(jnp.arange(ENTRIES // per_device))


def draw_query_bucket(key, part):
    positions = jnp.arange(QUERIES)
    column = positions // QUERY_DEV % N_LIB
    lower_upper = jax.random.randint(jax.random.fold_in(key, 11), (QUERIES,), 0, 2, dtype=jnp.int32)
    return (2 * column + lower_upper).astype(jnp.int32)


def draw_library_bucket(key, part):
    return (entry_permutations(key) % BUCKETS).reshape(ENTRIES).astype(jnp.int32)


def draw_library(key, part):
    library_base = jax.random.fold_in(key, 13)
    spectra_rows = jax.vmap(partial(raw_row, library_base))(jnp.arange(ENTRIES))
    return jnp.clip(spectra_rows, -64.0, 64.0).astype(jnp.bfloat16)


def draw_queries(key, part):
    query_base = jax.random.fold_in(key, 15)
    positions = jnp.arange(QUERIES)
    spectra_rows = jax.vmap(partial(raw_row, query_base))(positions)
    return jnp.clip(spectra_rows, -64.0, 64.0).astype(jnp.bfloat16)


def block_levels(rng, extent, cuts, low, largest):
    gain = 1.0
    for axis_at, blocks in cuts:
        heights = jax.random.uniform(jax.random.fold_in(jax.random.fold_in(rng, 6), axis_at), (blocks,), jnp.float32, low / len(cuts), largest / len(cuts))
        gain = gain * jnp.repeat(jnp.exp(heights), extent[axis_at] // blocks).reshape((-1,) + (1,) * (len(extent) - 1 - axis_at))
    return gain


def setup_inputs(seed: int = 0) -> dict:
    keys = jax.random.split(jax.random.key(seed), 6)
    queries = draw_queries(jax.random.fold_in(keys[5], 71), 0)
    query_bucket = draw_query_bucket(jax.random.fold_in(keys[5], 71), 0)
    library = draw_library(jax.random.fold_in(keys[5], 71), 0)
    library_time = jnp.clip(2.0 * jax.random.uniform(keys[3], (ENTRIES,), jnp.float32) ** block_levels(keys[3], (ENTRIES,), ((0, 128),), -0.2, 0.2), 0.0, 2.0).astype(jnp.bfloat16)
    library_bucket = draw_library_bucket(jax.random.fold_in(keys[5], 71), 0)
    return dict(queries=queries, query_bucket=query_bucket, library=library, library_time=library_time, library_bucket=library_bucket)


def entry_scale(spectra_rows):
    return lax.rsqrt(lax.optimization_barrier(jnp.mean(jnp.square(spectra_rows.astype(jnp.float32)), axis=1)) + 1e-06)

def reference(queries, query_bucket, library, library_time, library_bucket):
    library_scale = entry_scale(library)

    def one_block(inputs):
        query_block, block_bucket = inputs
        query_scale = entry_scale(query_block) * (SHARPNESS / BINS)
        products = lax.dot_general(query_block, library, (((1,), (1,)), ((), ())), preferred_element_type=jnp.float32)
        inside = jnp.abs(block_bucket[:, None] - library_bucket[None, :]) <= 1
        scores = jnp.where(inside, products * query_scale[:, None] * library_scale[None, :], -jnp.inf)
        maxima = lax.optimization_barrier(jnp.max(scores, axis=1))
        weights = jnp.exp(scores - maxima[:, None]).astype(jnp.bfloat16)
        totals = lax.optimization_barrier(jnp.sum(weights.astype(jnp.float32), axis=1))
        time_sum = jnp.dot(weights, library_time, preferred_element_type=jnp.float32)
        spectra_sum = jnp.dot(weights, library, preferred_element_type=jnp.float32)
        expected = (spectra_sum / totals[:, None]).astype(jnp.bfloat16)
        return (expected, time_sum / totals, maxima + jnp.log(totals))
    blocks = (queries.reshape(N_QUERY, BLOCK_ROWS, BINS), query_bucket.reshape(N_QUERY, BLOCK_ROWS))
    spectra, times, evidence = lax.map(one_block, blocks)
    return (spectra.reshape(QUERIES, BINS), times.reshape(QUERIES), evidence.reshape(QUERIES))
```

```python
import jax
import jax.numpy as jnp
from jax import lax
from jax.sharding import PartitionSpec as P

SHARPNESS = 448
PER_BUCKET = 12
N_LIB = 32


def entry_scale(spectra_rows):
    return lax.rsqrt(jnp.mean(jnp.square(spectra_rows.astype(jnp.float32)), axis=1) + 1e-06)


def bucket_positions(bucket):
    n = bucket.shape[0]
    at = jnp.arange(n)
    same = (bucket[None, :] == bucket[:, None]) & (at[None, :] < at[:, None])
    rank = jnp.sum(same.astype(jnp.int32), axis=1)
    return bucket * PER_BUCKET + rank


def per_device(queries, query_bucket, library, library_time, library_bucket):
    own_rows, bin_count = queries.shape
    lib_at = lax.axis_index("lib")
    positions = bucket_positions(library_bucket)
    row = jnp.arange(N_LIB * 48)
    wanted = (row // 48) * 24 - 12 + row % 48
    pick = (wanted[:, None] == positions[None, :]).astype(jnp.bfloat16)
    send = jnp.dot(pick, library, preferred_element_type=jnp.float32).astype(jnp.bfloat16)
    send_time = jnp.dot(pick, library_time, preferred_element_type=jnp.float32).astype(jnp.bfloat16)
    entries = lax.all_to_all(send.reshape(N_LIB, 48, bin_count), "lib", 0, 0).reshape(N_LIB * 48, bin_count)
    entry_time = lax.all_to_all(send_time.reshape(N_LIB, 48), "lib", 0, 0).reshape(N_LIB * 48)
    query_block = lax.all_gather(queries, "query", axis=0, tiled=True)
    block_bucket = lax.all_gather(query_bucket, "query", axis=0, tiled=True)
    query_scale = entry_scale(query_block) * (SHARPNESS / bin_count)
    products = lax.dot_general(query_block, entries, (((1,), (1,)), ((), ())), preferred_element_type=jnp.float32)
    row_bucket = 2 * lib_at - 1 + (row % 48) // PER_BUCKET
    inside = jnp.abs(block_bucket[:, None] - row_bucket[None, :]) <= 1
    inside = inside & (row_bucket >= 0)[None, :] & (row_bucket < 2 * N_LIB)[None, :]
    scores = jnp.where(inside, products * query_scale[:, None] * entry_scale(entries)[None, :], -jnp.inf)
    maxima = lax.pmax(jnp.max(scores, axis=1), "query")
    weights = jnp.exp(scores - maxima[:, None]).astype(jnp.bfloat16)
    total_part = jnp.sum(weights.astype(jnp.float32), axis=1)
    spectra_part = jnp.dot(weights, entries, preferred_element_type=jnp.float32)
    time_part = jnp.dot(weights, entry_time, preferred_element_type=jnp.float32)
    total_all, time_all = lax.psum((total_part, time_part), "query")
    spectra_sum = lax.psum_scatter(spectra_part, "query", scatter_dimension=0, tiled=True)
    first_row = lax.axis_index("query") * own_rows
    totals = lax.dynamic_slice_in_dim(total_all, first_row, own_rows)
    time_sum = lax.dynamic_slice_in_dim(time_all, first_row, own_rows)
    own_maxima = lax.dynamic_slice_in_dim(maxima, first_row, own_rows)
    expected = (spectra_sum / totals[:, None]).astype(jnp.bfloat16)
    return (expected, time_sum / totals, own_maxima + jnp.log(totals))


def solution(mesh):
    placed = (
        P(("query", "lib"), None),
        P(("query", "lib")),
        P(("lib", "query"), None),
        P(("lib", "query")),
        P(("lib", "query")),
    )
    return jax.shard_map(
        per_device,
        mesh=mesh,
        in_specs=placed,
        out_specs=(P(("query", "lib"), None), P(("query", "lib")), P(("query", "lib"))),
        check_vma=False,
    )
```
